32 devices in a mesh: pipe: 4 (over z), dp: 8 (over y, x, core).
Axes of the slice: x: 2, y: 2, z: 4, core: 2. Of those that a mesh axis runs over, the one named last changes fastest.
Arguments:
- grads: bfloat16 [4, 8, 192, 12288], P('pipe', 'dp'), may hold values from -24 to 24
- tied_grads: bfloat16 [4, 8, 128, 12288], P('pipe', 'dp'), may hold values from -24 to 24
- owned_blocks: int32 [4, 48], P('pipe'), may hold values from 0 to 47, each once within a row
- layer_counts: int32 [4], P('pipe'), may hold values from 2 to 4, as said below
- master: float32 [4, 192, 12288], P('pipe', 'dp'), may hold values from -6 to 6
- moment: float32 [4, 192, 12288], P('pipe', 'dp'), may hold values from -6 to 6
- second: float32 [4, 192, 12288], P('pipe', 'dp'), may hold values from 0.1 to 4
- tied_master: float32 [4, 64, 12288], P('pipe', 'dp'), may hold values from -6 to 6
- tied_moment: float32 [4, 64, 12288], P('pipe', 'dp'), may hold values from -6 to 6
- tied_second: float32 [4, 64, 12288], P('pipe', 'dp'), may hold values from 0.1 to 4
Outputs:
- new_master: float32 [4, 192, 12288], P('pipe', 'dp')
- new_moment: float32 [4, 192, 12288], P('pipe', 'dp')
- new_second: float32 [4, 192, 12288], P('pipe', 'dp')
- weights: bfloat16 [4, 192, 12288], P('pipe')
- tied_new_master: float32 [4, 64, 12288], P('pipe', 'dp')
- tied_new_moment: float32 [4, 64, 12288], P('pipe', 'dp')
- tied_new_second: float32 [4, 64, 12288], P('pipe', 'dp')
- tied_weights: bfloat16 [4, 128, 12288], P('pipe')
The draws below stay inside these ranges and needn't reach their ends.
Inputs may be any that keep to these rules, and one draw needn't show every extreme that they name: Each row of owned_blocks lists every block number once; the block at position k is owned by data-parallel rank k // 6. `layer_counts`: every section has at least two layers; some section has the most and some the fewest.
All inputs are finite; a program needn't handle non-finite values.
Results may differ from the reference program's by a relative error of at most 0.0065.
Values may be sent and summed in bfloat16 or wider, within the bound.
No kernel may reach another device: no remote copies, remote signals or barrier semaphores. Data moves between devices by JAX's collectives and lax.ppermute only.
A program may use at most 128 MiB of HBM per device.

```python
import math
import jax
import jax.numpy as jnp
from jax import lax

D = 12288
LSLOT = 4
ROWS = 48
BROWS = 4
EROWS = 128
SLAB = 192
NB = 48
HALF_ROWS = 64
N_PIPE = 4
N_DP = 8


def draw_layer_counts(key, part):
    counts = jax.random.randint(key, (N_PIPE,), 2, LSLOT + 1)
    section_order = jax.random.permutation(jax.random.fold_in(key, 7), N_PIPE)
    counts = counts.at[section_order[0]].set(LSLOT)
    counts = counts.at[section_order[1]].set(2)
    return counts.astype(jnp.int32)


def raised(array, rng, source, target, blocks, factor):
    owner, partner = [(jnp.arange(array.shape[position]) // (array.shape[position] // blocks)).reshape([-1 if axis == position else 1 for axis in range(array.ndim)]) for position in (source, target)]
    chosen = jax.random.permutation(rng, blocks)[partner]
    strong = (owner == chosen) | (owner == (partner + blocks // 2) % blocks)
    return jnp.where(strong, factor * array, array)


def block_levels(rng, dims, cuts, least, high):
    factor_of = 1.0
    for dim, blocks in cuts:
        draws = jax.random.uniform(jax.random.fold_in(jax.random.fold_in(rng, 6), dim), (blocks,), jnp.float32, least / len(cuts), high / len(cuts))
        factor_of = factor_of * jnp.repeat(jnp.exp(draws), dims[dim] // blocks).reshape((-1,) + (1,) * (len(dims) - 1 - dim))
    return factor_of


def centred(own_key, dims, spread, bound, pieces=(), dtype=jnp.bfloat16):
    loudness = block_levels(own_key, dims, pieces, -0.22, 0.18) if pieces else 1.0
    array = jax.random.normal(own_key, dims, jnp.float32) * spread * loudness
    return jnp.minimum(jnp.maximum(array, -bound), bound).astype(dtype)


def heavy_noise(key, dims, deviation, reach, split, heavy, dtype=jnp.bfloat16):
    drawn = deviation * jax.random.normal(key, dims, jnp.float32)
    if split:
        drawn = drawn * block_levels(key, dims, split, -0.22, 0.18)
    return jnp.clip(raised(drawn, jax.random.fold_in(key, 3), *heavy), -reach, reach).astype(dtype)


def setup_inputs(seed: int = 0) -> dict:
    key_of = jax.random.split(jax.random.key(seed), 11)
    return {
        "grads": heavy_noise(key_of[0], (N_PIPE, N_DP, SLAB, D), 4.0, 24.0, ((0, 4), (1, 8)), (1, 2, 8, 2.0)),
        "tied_grads": heavy_noise(key_of[1], (N_PIPE, N_DP, EROWS, D), 4.0, 24.0, ((0, 4), (1, 8)), (1, 2, 8, 2.0)),
        "owned_blocks": jax.vmap(lambda own: jax.random.permutation(own, NB))(jax.random.split(key_of[2], N_PIPE)).reshape((N_PIPE, NB)).astype(jnp.int32),
        "layer_counts": draw_layer_counts(jax.random.fold_in(key_of[10], 71), 0),
        "master": centred(key_of[4], (N_PIPE, SLAB, D), 1.0, 6.0, ((0, 4), (1, 8)), jnp.float32),
        "moment": centred(key_of[5], (N_PIPE, SLAB, D), 1.0, 6.0, ((0, 4), (1, 8)), jnp.float32),
        "second": jnp.clip(jnp.exp(math.log(4.0) - 3.6888794 * jax.random.uniform(key_of[6], (N_PIPE, SLAB, D), jnp.float32) ** block_levels(key_of[6], (N_PIPE, SLAB, D), ((0, 4), (1, 8)), -0.2, 0.2)), 0.1, 4.0),
        "tied_master": centred(key_of[7], (N_PIPE, HALF_ROWS, D), 1.0, 6.0, ((0, 4), (1, 8)), jnp.float32),
        "tied_moment": centred(key_of[8], (N_PIPE, HALF_ROWS, D), 1.0, 6.0, ((0, 4), (1, 8)), jnp.float32),
        "tied_second": jnp.clip(jnp.exp(math.log(4.0) - 3.6888794 * jax.random.uniform(key_of[9], (N_PIPE, HALF_ROWS, D), jnp.float32) ** block_levels(key_of[9], (N_PIPE, HALF_ROWS, D), ((0, 4), (1, 8)), -0.2, 0.2)), 0.1, 4.0),
    }


BETA_FIRST = 0.9
BETA_SECOND = 0.95
EPSILON = 1e-08
STEP_RATE = 0.05
WEIGHT_DECAY = 0.1

def adam_update(gradient, master_rows, moment_rows, second_rows, live_rows):
    moment_next = BETA_FIRST * moment_rows + (1.0 - BETA_FIRST) * gradient
    second_next = BETA_SECOND * second_rows + (1.0 - BETA_SECOND) * gradient * gradient
    update = moment_next / (jnp.sqrt(second_next) + EPSILON) + WEIGHT_DECAY * master_rows
    master_next = master_rows - STEP_RATE * update
    return (jnp.where(live_rows, master_next, master_rows), jnp.where(live_rows, moment_next, moment_rows), jnp.where(live_rows, second_next, second_rows))

def reference(grads, tied_grads, owned_blocks, layer_counts, master, moment, second, tied_master, tied_moment, tied_second):
    masters, moments, seconds, weight_list = ([], [], [], [])
    for section in range(N_PIPE):
        total = lax.optimization_barrier(jnp.sum(grads[section].astype(jnp.float32), axis=0)) / N_DP
        order_ids = owned_blocks[section]
        arranged = total.reshape(NB, BROWS, D)[order_ids].reshape(SLAB, D)
        live_rows = jnp.repeat(order_ids * BROWS // ROWS < layer_counts[section], BROWS)[:, None]
        master_next, moment_next, second_next = adam_update(arranged, master[section], moment[section], second[section], live_rows)
        rounded = master_next.astype(jnp.bfloat16).reshape(NB, BROWS, D)
        restored = jnp.zeros((NB, BROWS, D), jnp.bfloat16).at[order_ids].set(rounded).reshape(SLAB, D)
        masters.append(master_next)
        moments.append(moment_next)
        seconds.append(second_next)
        weight_list.append(restored)
    tied_totals = [lax.optimization_barrier(jnp.sum(tied_grads[section].astype(jnp.float32), axis=0)) for section in range(N_PIPE)]
    group_rows = HALF_ROWS // N_DP
    tied_masters, tied_moments, tied_seconds, tied_rounded = ([], [], [], [])
    for section in range(N_PIPE):
        partner_section = N_PIPE - 1 - section
        side_index = 0 if section < N_PIPE // 2 else 1
        joined = (tied_totals[section] + tied_totals[partner_section]) / N_DP
        mine_rows = joined.reshape(N_DP, 2, group_rows, D)[:, side_index].reshape(HALF_ROWS, D)
        master_next, moment_next, second_next = adam_update(mine_rows, tied_master[section], tied_moment[section], tied_second[section], True)
        tied_masters.append(master_next)
        tied_moments.append(moment_next)
        tied_seconds.append(second_next)
        tied_rounded.append(master_next.astype(jnp.bfloat16))
    tied_list = []
    for section in range(N_PIPE):
        partner_section = N_PIPE - 1 - section
        lower_section = min(section, partner_section)
        upper_section = max(section, partner_section)
        lower_half = tied_rounded[lower_section].reshape(N_DP, group_rows, D)
        upper_half = tied_rounded[upper_section].reshape(N_DP, group_rows, D)
        tied_list.append(jnp.stack((lower_half, upper_half), axis=1).reshape(EROWS, D))
    return (jnp.stack(masters), jnp.stack(moments), jnp.stack(seconds), jnp.stack(weight_list), jnp.stack(tied_masters), jnp.stack(tied_moments), jnp.stack(tied_seconds), jnp.stack(tied_list))
```

```python
import functools

import jax
import jax.numpy as jnp
from jax import lax
from jax.experimental import pallas as pl
from jax.experimental.pallas import tpu as pltpu
from jax.sharding import PartitionSpec as P

ROWS = 48
LANES = 128
SUBLANES = 8

BETA_FIRST = 0.9
BETA_SECOND = 0.95
EPSILON = 1e-08
STEP_RATE = 0.05
WEIGHT_DECAY = 0.1


F32 = jnp.float32
BF16 = jnp.bfloat16
VMEM = pl.BlockSpec(memory_space=pltpu.VMEM)
ANY = pl.BlockSpec(memory_space=pl.ANY)


def adam(gradient, master, moment, second):
    moment_next = BETA_FIRST * moment + (1.0 - BETA_FIRST) * gradient
    second_next = BETA_SECOND * second + (1.0 - BETA_SECOND) * gradient * gradient
    update = moment_next / (jnp.sqrt(second_next) + EPSILON) + WEIGHT_DECAY * master
    return master - STEP_RATE * update, moment_next, second_next


def parent_of(slot, colour):
    hop = 1 << (slot.bit_length() - 1) if colour == 0 else slot & -slot
    return slot ^ hop, hop


def link_slots(replicas):
    return sorted((j for j in range(replicas) if not j & 1), key=lambda j: (bin(j).count("1"), j))


def across(payload, hop):
    count = lax.axis_size("dp")
    return lax.ppermute(payload, "dp", [(i, i ^ hop) for i in range(count)])


def mirrored(payload):
    count = lax.axis_size("pipe")
    return lax.ppermute(payload, "pipe", [(i, count - 1 - i) for i in range(count)])


def block_view(rows2d, block_rows):
    rows, cols = rows2d.shape
    per = SUBLANES // block_rows if rows % SUBLANES == 0 else 1
    shaped = rows2d.reshape(rows // (per * block_rows), per, block_rows, cols // LANES, LANES)
    return shaped.transpose(0, 3, 1, 2, 4)


def flat_view(blocks):
    tiles, lane_tiles, per, block_rows, lanes = blocks.shape
    return blocks.transpose(0, 2, 3, 1, 4).reshape(tiles * per * block_rows, lane_tiles * lanes)


def pack_blocks(order, source, slots, owned, block_rows):
    view = block_view(source, block_rows)
    per, lane_tiles = view.shape[2], view.shape[1]
    half = lane_tiles // 2
    total = len(slots) * owned
    shape = jax.ShapeDtypeStruct((total // per, half, per, block_rows, LANES), source.dtype)

    def kernel(order_ref, src, first, last, sems):
        me = lax.axis_index("dp")
        for part, out in enumerate((first, last)):
            for s, slot in enumerate(slots):
                owner = me ^ slot
                for p in range(owned):
                    block = order_ref[owner * owned + p]
                    q = s * owned + p
                    pltpu.make_async_copy(
                        src.at[block // per, pl.ds(part * half, half), block % per],
                        out.at[q // per, :, q % per],
                        sems.at[part],
                    ).start()
        for part, out in enumerate((first, last)):
            pltpu.make_async_copy(out, out, sems.at[part]).wait()

    outs = pl.pallas_call(
        kernel,
        out_shape=(shape, shape),
        grid_spec=pltpu.PrefetchScalarGridSpec(
            num_scalar_prefetch=1,
            grid=(),
            in_specs=[ANY],
            out_specs=(VMEM, VMEM),
            scratch_shapes=[pltpu.SemaphoreType.DMA((2,))],
        ),
        name="pack_blocks",
    )(order, view)
    return [flat_view(o) for o in outs]


def pack_groups(source, slots, group):
    rows, cols = source.shape
    half = cols // 2
    shape = jax.ShapeDtypeStruct((len(slots) * group, half), source.dtype)

    def kernel(src, first, last, sems):
        me = lax.axis_index("dp")
        for part, out in enumerate((first, last)):
            for s, slot in enumerate(slots):
                start = pl.multiple_of((me ^ slot) * group, group)
                pltpu.make_async_copy(
                    src.at[pl.ds(start, group), pl.ds(part * half, half)],
                    out.at[pl.ds(s * group, group), :],
                    sems.at[part],
                ).start()
        for part, out in enumerate((first, last)):
            pltpu.make_async_copy(out, out, sems.at[part]).wait()

    return pl.pallas_call(
        kernel,
        out_shape=(shape, shape),
        in_specs=[ANY],
        out_specs=(VMEM, VMEM),
        scratch_shapes=[pltpu.SemaphoreType.DMA((2,))],
        name="pack_groups",
    )(source)


def chunk_of(cols, most=1024):
    width = LANES
    while width * 2 <= most and cols % (width * 2) == 0:
        width *= 2
    return width


def core_sum(kept, received, count):
    rows, cols = kept[0].shape
    each = rows // count
    if each % SUBLANES:
        sums = [(k.astype(F32) + r.astype(F32)).astype(BF16) for k, r in zip(kept, received)]
        return [[s[i * each : (i + 1) * each] for i in range(count)] for s in sums]
    width = chunk_of(cols, 512)
    colours = len(kept)

    def kernel(*refs):
        keeps, recvs, outs = refs[:colours], refs[colours : 2 * colours], refs[2 * colours :]

        def step(i, carry):
            at = pl.ds(pl.multiple_of(i * width, width), width)
            for c in range(colours):
                for s in range(count):
                    here = pl.ds(s * each, each)
                    outs[c * count + s][:, at] = (keeps[c][here, at].astype(F32) + recvs[c][here, at].astype(F32)).astype(BF16)
            return carry

        lax.fori_loop(0, cols // width, step, 0)

    outs = pl.pallas_call(
        kernel,
        out_shape=[jax.ShapeDtypeStruct((each, cols), BF16)] * (colours * count),
        in_specs=[VMEM] * (2 * colours),
        out_specs=[VMEM] * (colours * count),
        name="core_sum",
    )(*kept, *received)
    return [list(outs[c * count : (c + 1) * count]) for c in range(colours)]


def added(base, extras):
    total = base.astype(F32)
    for e in extras:
        total = total + e.astype(F32)
    return total


def reduce_tree(parts, replicas, colour):
    slots = link_slots(replicas)
    own = dict(zip(slots, parts))
    arrived = {j: [] for j in slots}
    for slot in reversed(slots[1:]):
        parent, hop = parent_of(slot, colour)
        payload = own[slot]
        if arrived[slot]:
            payload = added(payload, arrived[slot]).astype(BF16)
        arrived[parent].append(across(payload, hop))
    return own[0], arrived[0]


def spread_tree(chunk, replicas, colour):
    slots = link_slots(replicas)
    held = {0: chunk}
    for slot in slots[1:]:
        parent, hop = parent_of(slot, colour)
        held[slot] = across(held[parent], hop)
    return [held[j] for j in slots]


def section_step(order, counts, gradients, states, colour, previous, block_rows, replicas):
    rows, half = gradients[0].shape
    width = chunk_of(half)
    steps = half // width
    n_grad = len(gradients)
    owned = rows // block_rows

    def kernel(order_ref, counts_ref, *refs):
        grads, refs = refs[:n_grad], refs[n_grad:]
        (master, moment, second), refs = refs[:3], refs[3:]
        new_master, new_moment, new_second, cast = refs[-4:]
        at = pl.ds(pl.multiple_of(pl.program_id(0) * width, width), width)
        total = grads[0][:, at].astype(F32)
        for g in grads[1:]:
            total = total + g[:, at].astype(F32)
        me = lax.axis_index("dp")
        place = lax.broadcasted_iota(jnp.int32, (rows, width), 0) // block_rows
        live = jnp.zeros((rows, width), jnp.int32)
        for p in range(owned):
            block = order_ref[me * owned + p]
            flag = (block * block_rows // ROWS < counts_ref[0]).astype(jnp.int32)
            live = jnp.where(place == p, flag, live)
        live = live > 0
        old = master[...], moment[...], second[...]
        new = adam(total * (1.0 / replicas), *old)
        a, b, c = (jnp.where(live, n, o) for n, o in zip(new, old))
        new_master[...] = a
        new_moment[...] = b
        new_second[...] = c
        cast[:, at] = a.astype(BF16)

    block = pl.BlockSpec((rows, width), lambda i, *_: (0, i + colour * steps))
    shape = jax.ShapeDtypeStruct(states[0].shape, F32)
    n_in = 2 + n_grad + 3
    outs = pl.pallas_call(
        kernel,
        out_shape=(shape, shape, shape, jax.ShapeDtypeStruct((rows, half), BF16)),
        grid_spec=pltpu.PrefetchScalarGridSpec(
            num_scalar_prefetch=2,
            grid=(steps,),
            in_specs=[VMEM] * n_grad + [block] * 3 + [ANY] * len(previous),
            out_specs=(block, block, block, VMEM),
        ),
        input_output_aliases={n_in + i: i for i in range(len(previous))},
        name="section_step",
    )(order, counts, *gradients, *states, *previous)
    return list(outs[:3]), outs[3]


def tied_sums(first, last, upper, group_rows):
    totals = [added(part[0], part[1]) for part in (first, last)]
    low = jnp.concatenate([t[:group_rows] for t in totals], axis=1)
    high = jnp.concatenate([t[group_rows:] for t in totals], axis=1)
    mine = jnp.where(upper, high, low)
    other = jnp.where(upper, low, high).astype(BF16)
    return mine, other


def put_blocks(order, chunks, slots, owned, block_rows, out_rows, previous):
    half = chunks[0][0].shape[1]
    lane_tiles = half // LANES
    flat = [block_view(c, block_rows) for part in chunks for c in part]
    per = flat[0].shape[2]
    per_out = SUBLANES // block_rows
    count = len(slots)
    shape = jax.ShapeDtypeStruct((out_rows // SUBLANES, 2 * lane_tiles, per_out, block_rows, LANES), BF16)

    def kernel(order_ref, *refs):
        ins, out, sems = refs[: len(flat)], refs[-2], refs[-1]
        me = lax.axis_index("dp")
        for i, src in enumerate(ins):
            part, slot = i // count, slots[i % count]
            for p in range(owned):
                block = order_ref[(me ^ slot) * owned + p]
                pltpu.make_async_copy(
                    src.at[p // per, :, p % per],
                    out.at[block // per_out, pl.ds(part * lane_tiles, lane_tiles), block % per_out],
                    sems.at[i],
                ).start()
        for i, src in enumerate(ins):
            pltpu.make_async_copy(src, src, sems.at[i]).wait()

    return pl.pallas_call(
        kernel,
        out_shape=shape,
        grid_spec=pltpu.PrefetchScalarGridSpec(
            num_scalar_prefetch=1,
            grid=(),
            in_specs=[VMEM] * len(flat) + [ANY] * len(previous),
            out_specs=ANY,
            scratch_shapes=[pltpu.SemaphoreType.DMA((len(flat),))],
        ),
        input_output_aliases={1 + len(flat): 0} if previous else {},
        name="put_blocks",
    )(order, *flat, *previous)


def put_groups(chunks, slots, out_rows, previous):
    group, half = chunks[0][0].shape
    flat = [c for part in chunks for c in part]
    count = len(slots)

    def kernel(*refs):
        ins, out, sems = refs[: len(flat)], refs[-2], refs[-1]
        me = lax.axis_index("dp")
        for i, src in enumerate(ins):
            part, slot = i // count, slots[i % count]
            start = pl.multiple_of((me ^ slot) * group, group)
            pltpu.make_async_copy(src, out.at[pl.ds(start, group), pl.ds(part * half, half)], sems.at[i]).start()
        for i, src in enumerate(ins):
            pltpu.make_async_copy(src, src, sems.at[i]).wait()

    return pl.pallas_call(
        kernel,
        out_shape=jax.ShapeDtypeStruct((out_rows, 2 * half), BF16),
        in_specs=[VMEM] * len(flat) + [ANY] * len(previous),
        out_specs=ANY,
        scratch_shapes=[pltpu.SemaphoreType.DMA((len(flat),))],
        input_output_aliases={len(flat): 0} if previous else {},
        name="put_groups",
    )(*flat, *previous)


def per_device(grads, tied_grads, owned_blocks, layer_counts, master, moment, second, tied_master, tied_moment, tied_second):
    replicas = lax.axis_size("dp")
    upper = lax.axis_index("pipe") >= lax.axis_size("pipe") // 2
    slab, tied = grads[0, 0], tied_grads[0, 0]
    slab_rows, cols = slab.shape
    order = owned_blocks[0]
    blocks = order.shape[0]
    block_rows, owned = slab_rows // blocks, blocks // replicas
    tied_rows = tied.shape[0]
    group = tied_rows // replicas
    group_rows = group // 2

    here = link_slots(replicas)
    there = [j | 1 for j in here]
    tied_send = pack_groups(tied, there, group)
    tied_got = [across(x, 1) for x in tied_send]
    slab_send = pack_blocks(order, slab, there, owned, block_rows)
    slab_got = [across(x, 1) for x in slab_send]
    tied_keep = pack_groups(tied, here, group)
    slab_keep = pack_blocks(order, slab, here, owned, block_rows)

    tied_parts = core_sum(tied_keep, tied_got, len(here))
    slab_parts = core_sum(slab_keep, slab_got, len(here))
    tied_ends = [reduce_tree(tied_parts[c], replicas, c) for c in (0, 1)]
    slab_ends = [reduce_tree(slab_parts[c], replicas, c) for c in (0, 1)]

    mine, other = tied_sums(*tied_ends, upper, group_rows)
    tied_gradient = (mine + mirrored(other).astype(F32)) / replicas
    tied_new = adam(tied_gradient, tied_master[0], tied_moment[0], tied_second[0])

    states, previous, casts = (master[0], moment[0], second[0]), [], []
    for c in (0, 1):
        own, arrived = slab_ends[c]
        previous, cast = section_step(order, layer_counts, [own, *arrived], states, c, previous, block_rows, replicas)
        casts.append(cast)
    slab_here = [spread_tree(casts[c], replicas, c) for c in (0, 1)]
    slab_there = [[across(x, 1) for x in part] for part in slab_here]
    restored = put_blocks(order, slab_here, here, owned, block_rows, slab_rows, [])
    restored = put_blocks(order, slab_there, there, owned, block_rows, slab_rows, [restored])

    tied_cast = tied_new[0].astype(BF16)
    tied_partner = mirrored(tied_cast)
    pair = jnp.concatenate([jnp.where(upper, tied_partner, tied_cast), jnp.where(upper, tied_cast, tied_partner)], axis=0)
    tied_here = [spread_tree(pair[:, c * cols // 2 : (c + 1) * cols // 2], replicas, c) for c in (0, 1)]
    tied_there = [[across(x, 1) for x in part] for part in tied_here]
    tied_full = put_groups(tied_here, here, tied_rows, [])
    tied_full = put_groups(tied_there, there, tied_rows, [tied_full])

    return (
        previous[0][None],
        previous[1][None],
        previous[2][None],
        flat_view(restored)[None],
        tied_new[0][None],
        tied_new[1][None],
        tied_new[2][None],
        tied_full[None],
    )


def solution(mesh):
    split = P("pipe", "dp", None)
    return jax.shard_map(
        per_device,
        mesh=mesh,
        in_specs=(P("pipe", "dp", None, None), P("pipe", "dp", None, None), P("pipe", None), P("pipe")) + (split,) * 6,
        out_specs=(split, split, split, P("pipe", None, None), split, split, split, P("pipe", None, None)),
        check_vma=False,
    )
```

```python
import jax
import jax.numpy as jnp
from jax import lax
from jax.experimental import pallas as pl
from jax.experimental.pallas import tpu as pltpu
from jax.sharding import PartitionSpec as P


ROWS = 48
LANES = 128
SUBLANES = 8

BETA_FIRST = 0.9
BETA_SECOND = 0.95
EPSILON = 1e-08
STEP_RATE = 0.05
WEIGHT_DECAY = 0.1


F32 = jnp.float32
BF16 = jnp.bfloat16
VMEM = pl.BlockSpec(memory_space=pltpu.VMEM)
ANY = pl.BlockSpec(memory_space=pl.ANY)


def in_vmem():
    return len(link_slots(lax.axis_size("dp"))) <= 4


def near(x):
    return pltpu.with_memory_space_constraint(x, pltpu.VMEM) if in_vmem() else x


def placed(shape, dtype):
    return pltpu.VMEM(shape, dtype) if in_vmem() else jax.ShapeDtypeStruct(shape, dtype)


def small():
    return pltpu.CompilerParams(vmem_limit_bytes=1 << 20) if in_vmem() else pltpu.CompilerParams()


def far(x):
    return pltpu.with_memory_space_constraint(x, pltpu.HBM)


def adam(gradient, master, moment, second):
    moment_next = BETA_FIRST * moment + (1.0 - BETA_FIRST) * gradient
    second_next = BETA_SECOND * second + (1.0 - BETA_SECOND) * gradient * gradient
    update = moment_next / (jnp.sqrt(second_next) + EPSILON) + WEIGHT_DECAY * master
    return master - STEP_RATE * update, moment_next, second_next


def parent_of(slot, colour):
    hop = 1 << (slot.bit_length() - 1) if colour == 0 else slot & -slot
    return slot ^ hop, hop


def link_slots(replicas):
    return sorted((j for j in range(replicas) if not j & 1), key=lambda j: (bin(j).count("1"), j))


def across(payload, hop):
    count = lax.axis_size("dp")
    return lax.ppermute(payload, "dp", [(i, i ^ hop) for i in range(count)])


def mirrored(payload):
    count = lax.axis_size("pipe")
    return lax.ppermute(payload, "pipe", [(i, count - 1 - i) for i in range(count)])


def block_view(rows2d, block_rows):
    rows, cols = rows2d.shape
    per = SUBLANES // block_rows if rows % SUBLANES == 0 else 1
    shaped = rows2d.reshape(rows // (per * block_rows), per, block_rows, cols // LANES, LANES)
    return shaped.transpose(0, 3, 1, 2, 4)


def flat_view(blocks):
    tiles, lane_tiles, per, block_rows, lanes = blocks.shape
    return blocks.transpose(0, 2, 3, 1, 4).reshape(tiles * per * block_rows, lane_tiles * lanes)


def pack_blocks(order, source, slots, owned, block_rows):
    view = block_view(source, block_rows)
    per, lane_tiles = view.shape[2], view.shape[1]
    half = lane_tiles // 2
    total = len(slots) * owned
    shape = placed((total // per, half, per, block_rows, LANES), source.dtype)

    def kernel(order_ref, src, first, last, sems):
        me = lax.axis_index("dp")
        for part, out in enumerate((first, last)):
            for s, slot in enumerate(slots):
                owner = me ^ slot
                for p in range(owned):
                    block = order_ref[owner * owned + p]
                    q = s * owned + p
                    pltpu.make_async_copy(
                        src.at[block // per, pl.ds(part * half, half), block % per],
                        out.at[q // per, :, q % per],
                        sems.at[part],
                    ).start()
        for part, out in enumerate((first, last)):
            pltpu.make_async_copy(out, out, sems.at[part]).wait()

    outs = pl.pallas_call(
        kernel,
        out_shape=(shape, shape),
        grid_spec=pltpu.PrefetchScalarGridSpec(
            num_scalar_prefetch=1,
            grid=(),
            in_specs=[ANY],
            out_specs=(VMEM, VMEM),
            scratch_shapes=[pltpu.SemaphoreType.DMA((2,))],
        ),
        compiler_params=small(),
        name="pack_blocks",
    )(order, far(view))
    return [flat_view(o) for o in outs]


def pack_groups(source, slots, group):
    cols = source.shape[1]

    def kernel(src, out, sem):
        me = lax.axis_index("dp")
        for s, slot in enumerate(slots):
            start = pl.multiple_of((me ^ slot) * group, group)
            pltpu.make_async_copy(src.at[pl.ds(start, group)], out.at[pl.ds(s * group, group)], sem).start()
        pltpu.make_async_copy(out, out, sem).wait()

    return pl.pallas_call(
        kernel,
        out_shape=placed((len(slots) * group, cols), source.dtype),
        in_specs=[ANY],
        out_specs=VMEM,
        scratch_shapes=[pltpu.SemaphoreType.DMA],
        compiler_params=small(),
        name="pack_groups",
    )(far(source))


def chunk_of(cols, most=1024):
    width = LANES
    while width * 2 <= most and cols % (width * 2) == 0:
        width *= 2
    return width


def core_sum(kept, received, count):
    rows, cols = kept[0].shape
    each = rows // count
    if each % SUBLANES:
        sums = [(k.astype(F32) + r.astype(F32)).astype(BF16) for k, r in zip(kept, received)]
        return [[s[i * each : (i + 1) * each] for i in range(count)] for s in sums]
    width = chunk_of(cols, 512)
    colours = len(kept)

    def kernel(*refs):
        keeps, recvs, outs = refs[:colours], refs[colours : 2 * colours], refs[2 * colours :]

        def step(i, carry):
            at = pl.ds(pl.multiple_of(i * width, width), width)
            for c in range(colours):
                for s in range(count):
                    here = pl.ds(s * each, each)
                    outs[c * count + s][:, at] = (keeps[c][here, at].astype(F32) + recvs[c][here, at].astype(F32)).astype(BF16)
            return carry

        lax.fori_loop(0, cols // width, step, 0)

    outs = pl.pallas_call(
        kernel,
        out_shape=[placed((each, cols), BF16)] * (colours * count),
        in_specs=[VMEM] * (2 * colours),
        out_specs=[VMEM] * (colours * count),
        compiler_params=small(),
        name="core_sum",
    )(*map(near, kept), *map(near, received))
    return [list(outs[c * count : (c + 1) * count]) for c in range(colours)]


def group_sum(source, received, slots, group):
    half = received.shape[1] // 2
    width = chunk_of(half, 512)
    count = len(slots)

    def kernel(src, got, *outs):
        me = lax.axis_index("dp")

        def step(i, carry):
            at = pl.ds(pl.multiple_of(i * width, width), width)
            for c in (0, 1):
                wide = pl.ds(pl.multiple_of(c * half + i * width, width), width)
                for s, slot in enumerate(slots):
                    rows = pl.ds(pl.multiple_of((me ^ slot) * group, group), group)
                    total = src[rows, wide].astype(F32) + got[s * group : (s + 1) * group, wide].astype(F32)
                    outs[c * count + s][:, at] = total.astype(BF16)
            return carry

        lax.fori_loop(0, half // width, step, 0)

    outs = pl.pallas_call(
        kernel,
        out_shape=[placed((group, half), BF16)] * (2 * count),
        in_specs=[VMEM] * 2,
        out_specs=[VMEM] * (2 * count),
        compiler_params=small(),
        name="group_sum",
    )(near(source), near(received))
    return [list(outs[:count]), list(outs[count:])]


def added(base, extras):
    total = base.astype(F32)
    for e in extras:
        total = total + e.astype(F32)
    return total


def section_step(order, counts, gradients, states, colour, block_rows, replicas):
    rows, half = gradients[0].shape
    width = chunk_of(half, 256)
    n_grad = len(gradients)
    owned = rows // block_rows

    def kernel(order_ref, counts_ref, *refs):
        grads, olds, news, cast = refs[:n_grad], refs[n_grad : n_grad + 3], refs[n_grad + 3 : n_grad + 6], refs[-1]
        me = lax.axis_index("dp")
        place = lax.broadcasted_iota(jnp.int32, (rows, width), 0) // block_rows
        live = jnp.zeros((rows, width), jnp.int32)
        for p in range(owned):
            block = order_ref[me * owned + p]
            flag = (block * block_rows // ROWS < counts_ref[0]).astype(jnp.int32)
            live = jnp.where(place == p, flag, live)
        live = live > 0

        def step(i, carry):
            at = pl.ds(pl.multiple_of(i * width, width), width)
            wide = pl.ds(pl.multiple_of(colour * half + i * width, width), width)
            total = grads[0][:, at].astype(F32)
            for g in grads[1:]:
                total = total + g[:, at].astype(F32)
            old = [r[:, wide] for r in olds]
            new = [jnp.where(live, n, o) for n, o in zip(adam(total * (1.0 / replicas), *old), old)]
            for ref, value in zip(news, new):
                ref[:, at] = value
            cast[:, at] = new[0].astype(BF16)
            return carry

        lax.fori_loop(0, half // width, step, 0)

    shape = placed((rows, half), F32)
    outs = pl.pallas_call(
        kernel,
        out_shape=(shape, shape, shape, placed((rows, half), BF16)),
        grid_spec=pltpu.PrefetchScalarGridSpec(
            num_scalar_prefetch=2,
            grid=(),
            in_specs=[VMEM] * (n_grad + 3),
            out_specs=[VMEM] * 4,
        ),
        compiler_params=small(),
        name="section_step",
    )(order, counts, *map(near, gradients), *map(near, states))
    return list(outs[:3]), outs[3]


def upper_side():
    return lax.axis_index("pipe") >= lax.axis_size("pipe") // 2


def tied_sums(first, last, group_rows):
    own, extras = zip(first, last)
    half = own[0].shape[1]
    n_extra = len(extras[0])
    if group_rows % SUBLANES:
        totals = [added(o, e) for o, e in zip(own, extras)]
        low = jnp.concatenate([t[:group_rows] for t in totals], axis=1)
        high = jnp.concatenate([t[group_rows:] for t in totals], axis=1)
        return jnp.where(upper_side(), high, low), jnp.where(upper_side(), low, high).astype(BF16)
    width = chunk_of(half, 512)

    def kernel(*refs):
        mine, other = refs[-2:]
        upper = upper_side()

        def step(i, carry):
            at = pl.ds(pl.multiple_of(i * width, width), width)
            for c in (0, 1):
                ins = refs[c * (1 + n_extra) : (c + 1) * (1 + n_extra)]
                total = added(ins[0][:, at], [r[:, at] for r in ins[1:]])
                low, high = total[:group_rows], total[group_rows:]
                wide = pl.ds(pl.multiple_of(c * half + i * width, width), width)
                mine[:, wide] = jnp.where(upper, high, low)
                other[:, wide] = jnp.where(upper, low, high).astype(BF16)
            return carry

        lax.fori_loop(0, half // width, step, 0)

    args = [x for o, e in zip(own, extras) for x in (o, *e)]
    return pl.pallas_call(
        kernel,
        out_shape=(placed((group_rows, 2 * half), F32), placed((group_rows, 2 * half), BF16)),
        in_specs=[VMEM] * len(args),
        out_specs=[VMEM] * 2,
        compiler_params=small(),
        name="tied_sums",
    )(*map(near, args))


def tied_step(mine, partner, states, replicas):
    rows, cols = mine.shape
    width = chunk_of(cols)

    def kernel(mine_ref, partner_ref, *refs):
        olds, news, cast = refs[:3], refs[3:6], refs[-1]

        def step(i, carry):
            at = pl.ds(pl.multiple_of(i * width, width), width)
            gradient = (mine_ref[:, at] + partner_ref[:, at].astype(F32)) * (1.0 / replicas)
            new = adam(gradient, *(r[:, at] for r in olds))
            for ref, value in zip(news, new):
                ref[:, at] = value
            cast[:, at] = new[0].astype(BF16)
            return carry

        lax.fori_loop(0, cols // width, step, 0)

    shape = placed((rows, cols), F32)
    outs = pl.pallas_call(
        kernel,
        out_shape=(shape, shape, shape, placed((rows, cols), BF16)),
        in_specs=[VMEM] * 5,
        out_specs=[VMEM] * 4,
        compiler_params=small(),
        name="tied_step",
    )(near(mine), near(partner), *map(near, states))
    return list(outs[:3]), outs[3]


def tied_pair(mine, partner):
    rows, cols = mine.shape
    half = cols // 2
    if rows % SUBLANES:
        low = jnp.where(upper_side(), partner, mine)
        high = jnp.where(upper_side(), mine, partner)
        pair = jnp.concatenate([low, high], axis=0)
        return pair[:, :half], pair[:, half:]

    def kernel(mine_ref, partner_ref, *outs):
        upper = upper_side()

        def write(low, high):
            for c, out in enumerate(outs):
                out[:rows, :] = low[:, c * half : (c + 1) * half]
                out[rows:, :] = high[:, c * half : (c + 1) * half]

        @pl.when(upper)
        def _():
            write(partner_ref, mine_ref)

        @pl.when(jnp.logical_not(upper))
        def _():
            write(mine_ref, partner_ref)

    shape = placed((2 * rows, half), BF16)
    return pl.pallas_call(
        kernel, out_shape=(shape, shape), in_specs=[VMEM] * 2, out_specs=[VMEM] * 2, compiler_params=small(), name="tied_pair"
    )(near(mine), near(partner))


def flush(news):
    flat = [x for parts in news for x in parts]
    spots = [(i, k) for i, parts in enumerate(news) for k in range(len(parts))]

    def kernel(*refs):
        ins, outs, sems = refs[: len(flat)], refs[len(flat) : -1], refs[-1]
        for n, (src, (i, k)) in enumerate(zip(ins, spots)):
            cols = src.shape[1]
            pltpu.make_async_copy(src, outs[i].at[:, pl.ds(k * cols, cols)], sems.at[n]).start()
        for n, src in enumerate(ins):
            pltpu.make_async_copy(src, src, sems.at[n]).wait()

    return pl.pallas_call(
        kernel,
        out_shape=[jax.ShapeDtypeStruct((parts[0].shape[0], sum(x.shape[1] for x in parts)), F32) for parts in news],
        in_specs=[VMEM] * len(flat),
        out_specs=[ANY] * len(news),
        scratch_shapes=[pltpu.SemaphoreType.DMA((len(flat),))],
        compiler_params=small(),
        name="flush",
    )(*map(near, flat))


def stack(chunks):
    rows, cols = chunks[0].shape
    if rows % SUBLANES:
        return jnp.concatenate(chunks, axis=0)
    width = chunk_of(cols, 512)

    def kernel(*refs):
        def step(i, carry):
            at = pl.ds(pl.multiple_of(i * width, width), width)
            for k, src in enumerate(refs[:-1]):
                refs[-1][k * rows : (k + 1) * rows, at] = src[:, at]
            return carry

        lax.fori_loop(0, cols // width, step, 0)

    return pl.pallas_call(
        kernel,
        out_shape=placed((rows * len(chunks), cols), BF16),
        in_specs=[VMEM] * len(chunks),
        out_specs=VMEM,
        compiler_params=small(),
        name="stack",
    )(*map(near, chunks))


def put(order, sources, write, out_shape, previous):
    n = len(sources)

    def kernel(order_ref, *refs):
        ins, out, sems = refs[:n], refs[-2], refs[-1]
        write(order_ref, ins, out, sems)
        for i, src in enumerate(ins):
            pltpu.make_async_copy(src, src, sems.at[i]).wait()

    return pl.pallas_call(
        kernel,
        out_shape=out_shape,
        grid_spec=pltpu.PrefetchScalarGridSpec(
            num_scalar_prefetch=1,
            grid=(),
            in_specs=[VMEM] * n + [ANY] * len(previous),
            out_specs=ANY,
            scratch_shapes=[pltpu.SemaphoreType.DMA((n,))],
        ),
        input_output_aliases={1 + n: 0} if previous else {},
        compiler_params=small(),
    )(order, *map(near, sources), *map(far, previous))


def put_blocks(order, sources, pieces, owned, block_rows, out_rows, previous=()):
    lane_tiles, per = sources[0].shape[1:3]
    per_out = SUBLANES // block_rows
    tiles = owned // per
    shape = jax.ShapeDtypeStruct((out_rows // SUBLANES, 2 * lane_tiles, per_out, block_rows, LANES), BF16)

    def write(order_ref, ins, out, sems):
        me = lax.axis_index("dp")
        for i, (src, parts) in enumerate(zip(ins, pieces)):
            for k, (part, slot) in enumerate(parts):
                for p in range(owned):
                    block = order_ref[(me ^ slot) * owned + p]
                    pltpu.make_async_copy(
                        src.at[k * tiles + p // per, :, p % per],
                        out.at[block // per_out, pl.ds(part * lane_tiles, lane_tiles), block % per_out],
                        sems.at[i],
                    ).start()

    return put(order, sources, write, shape, previous)


def put_groups(order, sources, pieces, group, out_rows, previous=()):
    half = sources[0].shape[1]

    def write(order_ref, ins, out, sems):
        me = lax.axis_index("dp")
        for i, (src, parts) in enumerate(zip(ins, pieces)):
            for k, (part, slot) in enumerate(parts):
                start = pl.multiple_of((me ^ slot) * group, group)
                pltpu.make_async_copy(
                    src.at[pl.ds(k * group, group), :], out.at[pl.ds(start, group), pl.ds(part * half, half)], sems.at[i]
                ).start()

    shape = jax.ShapeDtypeStruct((out_rows, 2 * half), BF16)
    return put(order, sources, write, shape, previous)


def join(bases, extras):
    rows, cols = bases[0].shape
    if rows % SUBLANES:
        return [added(b, e).astype(BF16) for b, e in zip(bases, extras)]
    width = chunk_of(cols, 512)
    args = [x for b, e in zip(bases, extras) for x in (b, *e)]

    def kernel(*refs):
        outs = refs[len(args) :]

        def step(i, carry):
            at = pl.ds(pl.multiple_of(i * width, width), width)
            k = 0
            for out, e in zip(outs, extras):
                ins = refs[k : k + 1 + len(e)]
                out[:, at] = added(ins[0][:, at], [r[:, at] for r in ins[1:]]).astype(BF16)
                k += 1 + len(e)
            return carry

        lax.fori_loop(0, cols // width, step, 0)

    return pl.pallas_call(
        kernel,
        out_shape=[placed((rows, cols), BF16)] * len(bases),
        in_specs=[VMEM] * len(args),
        out_specs=[VMEM] * len(bases),
        compiler_params=small(),
        name="join",
    )(*map(near, args))


def reduce_trees(parts, replicas):
    slots = link_slots(replicas)
    own = [dict(zip(slots, p)) for p in parts]
    arrived = [{j: [] for j in slots} for _ in parts]
    for level in range(max(bin(j).count("1") for j in slots), 0, -1):
        todo = [(c, j) for j in slots if bin(j).count("1") == level for c in range(len(parts))]
        mixed = [(c, j) for c, j in todo if arrived[c][j]]
        sums = dict(zip(mixed, join([own[c][j] for c, j in mixed], [arrived[c][j] for c, j in mixed]))) if mixed else {}
        for c, j in todo:
            parent, hop = parent_of(j, c)
            arrived[c][parent].append(across(sums.get((c, j), own[c][j]), hop))
    return [(own[c][0], arrived[c][0]) for c in range(len(parts))]


def spread_trees(chunks, replicas):
    slots = link_slots(replicas)
    got = {(c, 0): chunk for c, chunk in enumerate(chunks)}
    for slot in slots[1:]:
        for c in range(len(chunks)):
            parent, hop = parent_of(slot, c)
            got[c, slot] = across(got[c, parent], hop)
    return got


def body(grads, tied_grads, owned_blocks, layer_counts, master, moment, second, tied_master, tied_moment, tied_second):
    replicas = lax.axis_size("dp")
    slab, tied = grads[0, 0], tied_grads[0, 0]
    slab_rows = slab.shape[0]
    order = owned_blocks[0]
    blocks = order.shape[0]
    block_rows, owned = slab_rows // blocks, blocks // replicas
    tied_rows = tied.shape[0]
    group = tied_rows // replicas

    here = link_slots(replicas)
    there = [j | 1 for j in here]
    turns = [[j for j in here if j == here[-1]], [j for j in here if j != here[-1]]]
    tied_got = []
    for slots in turns:
        x = pack_groups(tied, [j | 1 for j in slots], group)
        tied_got.append(across(x, 1))
    slab_send = pack_blocks(order, slab, there, owned, block_rows)
    slab_got = []
    for x in slab_send:
        slab_got.append(across(x, 1))
    tied_parts = [[], []]
    for i, slots in enumerate(turns):
        for c, outs in enumerate(group_sum(tied, tied_got[i], slots, group)):
            tied_parts[c] = outs + tied_parts[c]
    slab_keep = pack_blocks(order, slab, here, owned, block_rows)
    slab_parts = core_sum(slab_keep, slab_got, len(here))
    tied_ends = reduce_trees(tied_parts, replicas)
    slab_ends = reduce_trees(slab_parts, replicas)

    mine, other = tied_sums(*tied_ends, group // 2)
    partner = mirrored(other)
    tied_states, tied_cast = tied_step(mine, partner, [x[0] for x in (tied_master, tied_moment, tied_second)], replicas)
    tied_partner = mirrored(tied_cast)
    pair = tied_pair(tied_cast, tied_partner)

    states, fresh, casts = [master[0], moment[0], second[0]], [], []
    for c in (0, 1):
        own, arrived = slab_ends[c]
        news, cast = section_step(order, layer_counts, [own, *arrived], states, c, block_rows, replicas)
        fresh.append(news)
        casts.append(cast)
    fresh = [[part[i] for part in fresh] for i in range(3)] + [[x] for x in tied_states]
    states = flush(fresh)
    slab_chunks = spread_trees(casts, replicas)
    tied_chunks = spread_trees(pair, replicas)

    def other(keys):
        return [(c, slot | 1) for c, slot in keys]

    keys = list(slab_chunks)
    chunks = [slab_chunks[k] for k in keys]
    x = stack(chunks)
    x = across(x, 1)
    views = [block_view(c, block_rows) for c in chunks]
    restored = put_blocks(order, views, [[k] for k in keys], owned, block_rows, slab_rows)
    restored = put_blocks(order, [block_view(x, block_rows)], [other(keys)], owned, block_rows, slab_rows, [restored])

    keys = list(tied_chunks)
    early, late = [k for k in keys if k[1] != here[-1]], [k for k in keys if k[1] == here[-1]]
    chunks = [tied_chunks[k] for k in early]
    x = stack(chunks)
    x = across(x, 1)
    tied_full = put_groups(order, [*chunks, x], [[k] for k in early] + [other(early)], group, tied_rows)
    chunks = [tied_chunks[k] for k in late]
    tied_full = put_groups(order, chunks, [[k] for k in late], group, tied_rows, [tied_full])
    brought = []
    for (c, _), x in zip(late, chunks):
        brought.append(across(x, 1))
    tied_full = put_groups(order, brought, [other([k]) for k in late], group, tied_rows, [tied_full])

    return (*(x[None] for x in states[:3]), flat_view(restored)[None], *(x[None] for x in states[3:]), tied_full[None])


def solution(mesh):
    split = P("pipe", "dp", None)
    step = jax.shard_map(
        body,
        mesh=mesh,
        in_specs=(P("pipe", "dp", None, None), P("pipe", "dp", None, None), P("pipe", None), P("pipe")) + (split,) * 6,
        out_specs=(split, split, split, P("pipe", None, None), split, split, split, P("pipe", None, None)),
        check_vma=False,
    )
    if len(link_slots(mesh.shape["dp"])) != 4:
        return step
    return step
```

```python
import jax
import jax.numpy as jnp
from jax import lax
from jax.experimental import pallas as pl
from jax.experimental.pallas import tpu as pltpu
from jax.sharding import PartitionSpec as P


ROWS = 48
LANES = 128
SUBLANES = 8

BETA_FIRST = 0.9
BETA_SECOND = 0.95
EPSILON = 1e-08
STEP_RATE = 0.05
WEIGHT_DECAY = 0.1


F32 = jnp.float32
BF16 = jnp.bfloat16
VMEM = pl.BlockSpec(memory_space=pltpu.VMEM)
ANY = pl.BlockSpec(memory_space=pl.ANY)
SMEM = pl.BlockSpec(memory_space=pltpu.SMEM)


def in_vmem():
    return len(link_slots(lax.axis_size("dp"))) <= 4


def near(x):
    return pltpu.with_memory_space_constraint(x, pltpu.VMEM) if in_vmem() else x


def scalars(x):
    return pltpu.with_memory_space_constraint(x, pltpu.SMEM) if in_vmem() else x


def placed(shape, dtype):
    return pltpu.VMEM(shape, dtype) if in_vmem() else jax.ShapeDtypeStruct(shape, dtype)


def small():
    return pltpu.CompilerParams(vmem_limit_bytes=1 << 20) if in_vmem() else pltpu.CompilerParams()


def far(x):
    return pltpu.with_memory_space_constraint(x, pltpu.HBM)


def adam(gradient, master, moment, second):
    moment_next = BETA_FIRST * moment + (1.0 - BETA_FIRST) * gradient
    second_next = BETA_SECOND * second + (1.0 - BETA_SECOND) * gradient * gradient
    update = moment_next / (jnp.sqrt(second_next) + EPSILON) + WEIGHT_DECAY * master
    return master - STEP_RATE * update, moment_next, second_next


def parent_of(slot, colour):
    hop = 1 << (slot.bit_length() - 1) if colour == 0 else slot & -slot
    return slot ^ hop, hop


def link_slots(replicas):
    return sorted((j for j in range(replicas) if not j & 1), key=lambda j: (bin(j).count("1"), j))


def across(payload, hop):
    count = lax.axis_size("dp")
    return lax.ppermute(payload, "dp", [(i, i ^ hop) for i in range(count)])


def mirrored(payload):
    count = lax.axis_size("pipe")
    return lax.ppermute(payload, "pipe", [(i, count - 1 - i) for i in range(count)])


def block_view(rows2d, block_rows):
    rows, cols = rows2d.shape
    per = SUBLANES // block_rows if rows % SUBLANES == 0 else 1
    shaped = rows2d.reshape(rows // (per * block_rows), per, block_rows, cols // LANES, LANES)
    return shaped.transpose(0, 3, 1, 2, 4)


def flat_view(blocks):
    tiles, lane_tiles, per, block_rows, lanes = blocks.shape
    return blocks.transpose(0, 2, 3, 1, 4).reshape(tiles * per * block_rows, lane_tiles * lanes)


def pack_blocks(order, source, lists, owned, block_rows):
    view = block_view(source, block_rows)
    lane_tiles, per = view.shape[1:3]
    totals = [len(slots) * owned for slots in lists]
    to = [per if t % per == 0 else 1 for t in totals]

    def kernel(order_ref, src, *refs):
        outs, sems = refs[:-1], refs[-1]
        me = lax.axis_index("dp")
        for n, (slots, out) in enumerate(zip(lists, outs)):
            for s, slot in enumerate(slots):
                for p in range(owned):
                    block = order_ref[(me ^ slot) * owned + p]
                    q = s * owned + p
                    pltpu.make_async_copy(src.at[block // per, :, block % per], out.at[q // to[n], :, q % to[n]], sems.at[n]).start()
        for n, out in enumerate(outs):
            pltpu.make_async_copy(out, out, sems.at[n]).wait()

    packed = pl.pallas_call(
        kernel,
        out_shape=[placed((t // k, lane_tiles, k, block_rows, LANES), source.dtype) for t, k in zip(totals, to)],
        in_specs=[SMEM, ANY],
        out_specs=[VMEM] * len(lists),
        scratch_shapes=[pltpu.SemaphoreType.DMA((len(lists),))],
        compiler_params=small(),
        name="pack_blocks",
    )(scalars(order), far(view))
    return [flat_view(x) for x in packed]


def pack_groups(source, lists, group):
    half = source.shape[1] // 2

    def kernel(src, *refs):
        outs, sems = refs[:-1], refs[-1]
        me = lax.axis_index("dp")
        for n, (entries, out) in enumerate(zip(lists, outs)):
            for k, (c, slot) in enumerate(entries):
                start = pl.multiple_of((me ^ slot) * group, group)
                pltpu.make_async_copy(
                    src.at[pl.ds(start, group), pl.ds(c * half, half)], out.at[pl.ds(k * group, group)], sems.at[n]
                ).start()
        for n, out in enumerate(outs):
            pltpu.make_async_copy(out, out, sems.at[n]).wait()

    return pl.pallas_call(
        kernel,
        out_shape=[placed((len(entries) * group, half), source.dtype) for entries in lists],
        in_specs=[ANY],
        out_specs=[VMEM] * len(lists),
        scratch_shapes=[pltpu.SemaphoreType.DMA((len(lists),))],
        compiler_params=small(),
        name="pack_groups",
    )(far(source))


def chunk_of(cols, most=1024):
    width = LANES
    while width * 2 <= most and cols % (width * 2) == 0:
        width *= 2
    return width


def core_sum(kept, received, count, parts=1):
    rows, cols = kept.shape
    each, cols = rows // count, cols // parts
    spots = [(c, k) for c in range(parts) for k in range(count)]
    if each % SUBLANES:
        total = (kept.astype(F32) + received.astype(F32)).astype(BF16)
        return [total[k * each : (k + 1) * each, c * cols : (c + 1) * cols] for c, k in spots]
    width = chunk_of(cols, 512)

    def kernel(keep, recv, *outs):
        def step(i, carry):
            at = pl.ds(pl.multiple_of(i * width, width), width)
            for out, (c, k) in zip(outs, spots):
                here = pl.ds(k * each, each), pl.ds(pl.multiple_of(c * cols + i * width, width), width)
                out[:, at] = (keep[here].astype(F32) + recv[here].astype(F32)).astype(BF16)
            return carry

        lax.fori_loop(0, cols // width, step, 0)

    return pl.pallas_call(
        kernel,
        out_shape=[placed((each, cols), BF16)] * len(spots),
        in_specs=[VMEM] * 2,
        out_specs=[VMEM] * len(spots),
        compiler_params=small(),
        name="core_sum",
    )(near(kept), near(received))


def settled(piece, rows):
    array, first = piece
    return (array[first : first + rows], 0) if rows % SUBLANES and array.shape[0] != rows else piece


def added(pieces, rows, at=slice(None)):
    total = None
    for array, first in pieces:
        part = array[first : first + rows, at].astype(F32)
        total = part if total is None else total + part
    return total


def within(refs, pieces):
    return [(ref, first) for ref, (_, first) in zip(refs, pieces)]


def section_step(order, counts, gradients, states, colour, block_rows, replicas):
    rows, half = gradients[0][0].shape
    gradients = [settled(g, rows) for g in gradients]
    width = chunk_of(half, 256)
    n_grad = len(gradients)
    owned = rows // block_rows

    def kernel(order_ref, counts_ref, *refs):
        grads, olds, news, cast = refs[:n_grad], refs[n_grad : n_grad + 3], refs[n_grad + 3 : n_grad + 6], refs[-1]
        me = lax.axis_index("dp")
        place = lax.broadcasted_iota(jnp.int32, (rows, width), 0) // block_rows
        live = jnp.zeros((rows, width), jnp.int32)
        for p in range(owned):
            block = order_ref[me * owned + p]
            flag = (block * block_rows // ROWS < counts_ref[0]).astype(jnp.int32)
            live = jnp.where(place == p, flag, live)
        live = live > 0

        def step(i, carry):
            at = pl.ds(pl.multiple_of(i * width, width), width)
            wide = pl.ds(pl.multiple_of(colour * half + i * width, width), width)
            total = added(within(grads, gradients), rows, at)
            old = [r[:, wide] for r in olds]
            new = [jnp.where(live, n, o) for n, o in zip(adam(total * (1.0 / replicas), *old), old)]
            for ref, value in zip(news, new):
                ref[:, at] = value
            cast[:, at] = new[0].astype(BF16)
            return carry

        lax.fori_loop(0, half // width, step, 0)

    shape = placed((rows, half), F32)
    outs = pl.pallas_call(
        kernel,
        out_shape=(shape, shape, shape, placed((rows, half), BF16)),
        in_specs=[SMEM] * 2 + [VMEM] * (n_grad + 3),
        out_specs=[VMEM] * 4,
        compiler_params=small(),
        name="section_step",
    )(scalars(order), scalars(counts), *(near(g) for g, _ in gradients), *map(near, states))
    return list(outs[:3]), outs[3]


def upper_side():
    return lax.axis_index("pipe") >= lax.axis_size("pipe") // 2


def tied_sums(first, last, group_rows):
    rows, half = first[0][0].shape
    parts = [[settled(p, rows) for p in pieces] for pieces in (first, last)]
    if group_rows % SUBLANES:
        totals = [added(pieces, rows) for pieces in parts]
        low = jnp.concatenate([t[:group_rows] for t in totals], axis=1)
        high = jnp.concatenate([t[group_rows:] for t in totals], axis=1)
        return jnp.where(upper_side(), high, low), jnp.where(upper_side(), low, high).astype(BF16)
    width = chunk_of(half, 512)
    count = len(parts[0])

    def kernel(*refs):
        mine, other = refs[-2:]
        upper = upper_side()

        def step(i, carry):
            at = pl.ds(pl.multiple_of(i * width, width), width)
            for c in (0, 1):
                total = added(within(refs[c * count : (c + 1) * count], parts[c]), rows, at)
                low, high = total[:group_rows], total[group_rows:]
                wide = pl.ds(pl.multiple_of(c * half + i * width, width), width)
                mine[:, wide] = jnp.where(upper, high, low)
                other[:, wide] = jnp.where(upper, low, high).astype(BF16)
            return carry

        lax.fori_loop(0, half // width, step, 0)

    args = [near(array) for pieces in parts for array, _ in pieces]
    return pl.pallas_call(
        kernel,
        out_shape=(placed((group_rows, 2 * half), F32), placed((group_rows, 2 * half), BF16)),
        in_specs=[VMEM] * len(args),
        out_specs=[VMEM] * 2,
        compiler_params=small(),
        name="tied_sums",
    )(*args)


def tied_step(mine, partner, states, replicas):
    rows, cols = mine.shape
    width = chunk_of(cols)

    def kernel(mine_ref, partner_ref, *refs):
        olds, news, cast = refs[:3], refs[3:6], refs[-1]

        def step(i, carry):
            at = pl.ds(pl.multiple_of(i * width, width), width)
            gradient = (mine_ref[:, at] + partner_ref[:, at].astype(F32)) * (1.0 / replicas)
            new = adam(gradient, *(r[:, at] for r in olds))
            for ref, value in zip(news, new):
                ref[:, at] = value
            cast[:, at] = new[0].astype(BF16)
            return carry

        lax.fori_loop(0, cols // width, step, 0)

    shape = placed((rows, cols), F32)
    outs = pl.pallas_call(
        kernel,
        out_shape=(shape, shape, shape, placed((rows, cols), BF16)),
        in_specs=[VMEM] * 5,
        out_specs=[VMEM] * 4,
        compiler_params=small(),
        name="tied_step",
    )(near(mine), near(partner), *map(near, states))
    return list(outs[:3]), outs[3]


def tied_pair(mine, partner):
    rows, cols = mine.shape
    half = cols // 2
    if rows % SUBLANES:
        low = jnp.where(upper_side(), partner, mine)
        high = jnp.where(upper_side(), mine, partner)
        pair = jnp.concatenate([low, high], axis=0)
        return pair[:, :half], pair[:, half:]

    def kernel(mine_ref, partner_ref, *outs):
        upper = upper_side()

        def write(low, high):
            for c, out in enumerate(outs):
                out[:rows, :] = low[:, c * half : (c + 1) * half]
                out[rows:, :] = high[:, c * half : (c + 1) * half]

        @pl.when(upper)
        def _():
            write(partner_ref, mine_ref)

        @pl.when(jnp.logical_not(upper))
        def _():
            write(mine_ref, partner_ref)

    shape = placed((2 * rows, half), BF16)
    return pl.pallas_call(
        kernel, out_shape=(shape, shape), in_specs=[VMEM] * 2, out_specs=[VMEM] * 2, compiler_params=small(), name="tied_pair"
    )(near(mine), near(partner))


def flush(news):
    flat = [x for parts in news for x in parts]
    spots = [(i, k) for i, parts in enumerate(news) for k in range(len(parts))]

    def kernel(*refs):
        ins, outs, sems = refs[: len(flat)], refs[len(flat) : -1], refs[-1]
        for n, (src, (i, k)) in enumerate(zip(ins, spots)):
            cols = src.shape[1]
            pltpu.make_async_copy(src, outs[i].at[:, pl.ds(k * cols, cols)], sems.at[n]).start()
        for n, src in enumerate(ins):
            pltpu.make_async_copy(src, src, sems.at[n]).wait()

    return pl.pallas_call(
        kernel,
        out_shape=[jax.ShapeDtypeStruct((parts[0].shape[0], sum(x.shape[1] for x in parts)), F32) for parts in news],
        in_specs=[VMEM] * len(flat),
        out_specs=[ANY] * len(news),
        scratch_shapes=[pltpu.SemaphoreType.DMA((len(flat),))],
        compiler_params=small(),
        name="flush",
    )(*map(near, flat))


def stack(chunks):
    rows, cols = chunks[0].shape
    if rows % SUBLANES:
        return jnp.concatenate(chunks, axis=0)
    width = chunk_of(cols, 512)

    def kernel(*refs):
        def step(i, carry):
            at = pl.ds(pl.multiple_of(i * width, width), width)
            for k, src in enumerate(refs[:-1]):
                refs[-1][k * rows : (k + 1) * rows, at] = src[:, at]
            return carry

        lax.fori_loop(0, cols // width, step, 0)

    return pl.pallas_call(
        kernel,
        out_shape=placed((rows * len(chunks), cols), BF16),
        in_specs=[VMEM] * len(chunks),
        out_specs=VMEM,
        compiler_params=small(),
        name="stack",
    )(*map(near, chunks))


def put(orders, sources, write, out_shape, previous):
    n, lead = len(sources), len(orders)

    def kernel(*refs):
        ins, out, sems = refs[lead : lead + n], refs[-2], refs[-1]
        write(*refs[:lead], ins, out, sems)
        for i, src in enumerate(ins):
            pltpu.make_async_copy(src, src, sems.at[i]).wait()

    return pl.pallas_call(
        kernel,
        out_shape=out_shape,
        in_specs=[SMEM] * lead + [VMEM] * n + [ANY] * len(previous),
        out_specs=ANY,
        scratch_shapes=[pltpu.SemaphoreType.DMA((n,))],
        input_output_aliases={lead + n: 0} if previous else {},
        compiler_params=small(),
    )(*map(scalars, orders), *map(near, sources), *map(far, previous))


def put_blocks(order, sources, pieces, owned, block_rows, out_rows, previous=()):
    lane_tiles, per = sources[0].shape[1:3]
    per_out = SUBLANES // block_rows
    tiles = owned // per
    shape = jax.ShapeDtypeStruct((out_rows // SUBLANES, 2 * lane_tiles, per_out, block_rows, LANES), BF16)

    def write(order_ref, ins, out, sems):
        me = lax.axis_index("dp")
        for i, (src, parts) in enumerate(zip(ins, pieces)):
            for k, (part, slot) in enumerate(parts):
                for p in range(owned):
                    block = order_ref[(me ^ slot) * owned + p]
                    pltpu.make_async_copy(
                        src.at[k * tiles + p // per, :, p % per],
                        out.at[block // per_out, pl.ds(part * lane_tiles, lane_tiles), block % per_out],
                        sems.at[i],
                    ).start()

    return put([order], sources, write, shape, previous)


def put_groups(sources, pieces, group, out_rows, previous=()):
    half = sources[0].shape[1]

    def write(ins, out, sems):
        me = lax.axis_index("dp")
        for i, (src, parts) in enumerate(zip(ins, pieces)):
            for k, (part, slot) in enumerate(parts):
                start = pl.multiple_of((me ^ slot) * group, group)
                pltpu.make_async_copy(
                    src.at[pl.ds(k * group, group), :], out.at[pl.ds(start, group), pl.ds(part * half, half)], sems.at[i]
                ).start()

    shape = jax.ShapeDtypeStruct((out_rows, 2 * half), BF16)
    return put([], sources, write, shape, previous)


def join(sums, rows):
    cols = sums[0][0][0].shape[1]
    sums = [[settled(p, rows) for p in pieces] for pieces in sums]
    if rows % SUBLANES:
        return [added(pieces, rows).astype(BF16) for pieces in sums]
    width = chunk_of(cols, 512)
    args = [near(array) for pieces in sums for array, _ in pieces]

    def kernel(*refs):
        outs = refs[len(args) :]

        def step(i, carry):
            at = pl.ds(pl.multiple_of(i * width, width), width)
            k = 0
            for out, pieces in zip(outs, sums):
                out[:, at] = added(within(refs[k : k + len(pieces)], pieces), rows, at).astype(BF16)
                k += len(pieces)
            return carry

        lax.fori_loop(0, cols // width, step, 0)

    return pl.pallas_call(
        kernel,
        out_shape=[placed((rows, cols), BF16)] * len(sums),
        in_specs=[VMEM] * len(args),
        out_specs=[VMEM] * len(sums),
        compiler_params=small(),
        name="join",
    )(*args)


def leaves_of(slots, colour):
    parents = {parent_of(j, colour)[0] for j in slots if j}
    found = [j for j in reversed(slots) if j not in parents]
    return found, parent_of(found[0], colour)[1]


def reduce_trees(own, merged, slots, rows):
    arrived = {(c, j): [] for c in (0, 1) for j in slots}
    for c, array in enumerate(merged):
        found, hop = leaves_of(slots, c)
        got = across(array, hop)
        for k, j in enumerate(found):
            arrived[c, parent_of(j, c)[0]].append((got, k * rows))
    for level in range(max(bin(j).count("1") for j in slots), 0, -1):
        todo = [(c, j) for j in slots if bin(j).count("1") == level for c in (0, 1) if (c, j) in own]
        mixed = [k for k in todo if arrived[k]]
        if mixed:
            own.update(zip(mixed, join([[(own[k], 0), *arrived[k]] for k in mixed], rows)))
        for c, j in todo:
            parent, hop = parent_of(j, c)
            arrived[c, parent].append((across(own[c, j], hop), 0))
    return [[(own[c, 0], 0), *arrived[c, 0]] for c in (0, 1)]


def spread_trees(chunks, replicas):
    slots = link_slots(replicas)
    got = {(c, 0): chunk for c, chunk in enumerate(chunks)}
    for slot in slots[1:]:
        for c in range(len(chunks)):
            parent, hop = parent_of(slot, c)
            got[c, slot] = across(got[c, parent], hop)
    return got


def body(grads, tied_grads, owned_blocks, layer_counts, master, moment, second, tied_master, tied_moment, tied_second):
    replicas = lax.axis_size("dp")
    slab, tied = grads[0, 0], tied_grads[0, 0]
    slab_rows = slab.shape[0]
    order = owned_blocks[0]
    blocks = order.shape[0]
    block_rows, owned = slab_rows // blocks, blocks // replicas
    tied_rows = tied.shape[0]
    group = tied_rows // replicas

    here = link_slots(replicas)
    leaves = [[(c, j) for j in leaves_of(here, c)[0]] for c in (0, 1)]
    entries = [*leaves, [(c, j) for c in (0, 1) for j in here if (c, j) not in leaves[c]]]
    tied_sum = []
    for i, keys in enumerate(entries):
        x, kept = pack_groups(tied, [[(c, j | 1) for c, j in keys], keys], group)
        x = across(x, 1)
        tied_sum.append(core_sum(kept, x, 1 if i < 2 else len(keys)))
    tied_own = dict(zip(entries[2], tied_sum[2]))
    tied_ends = reduce_trees(tied_own, [x[0] for x in tied_sum[:2]], here, group)

    slab_own = {}
    for slots in ([here[-1]], here[:-1]):
        x, kept = pack_blocks(order, slab, [[j | 1 for j in slots], slots], owned, block_rows)
        x = across(x, 1)
        keys = [(c, j) for c in (0, 1) for j in slots]
        slab_own.update(zip(keys, core_sum(kept, x, len(slots), 2)))
    slab_ends = reduce_trees(slab_own, [], here, owned * block_rows)

    mine, other = tied_sums(*tied_ends, group // 2)
    partner = mirrored(other)
    tied_states, tied_cast = tied_step(mine, partner, [x[0] for x in (tied_master, tied_moment, tied_second)], replicas)
    tied_partner = mirrored(tied_cast)
    pair = tied_pair(tied_cast, tied_partner)

    states, fresh, casts = [master[0], moment[0], second[0]], [], []
    for c in (0, 1):
        news, cast = section_step(order, layer_counts, slab_ends[c], states, c, block_rows, replicas)
        fresh.append(news)
        casts.append(cast)
    fresh = [[part[i] for part in fresh] for i in range(3)] + [[x] for x in tied_states]
    states = flush(fresh)
    slab_chunks = spread_trees(casts, replicas)
    tied_chunks = spread_trees(pair, replicas)

    def other(keys):
        return [(c, slot | 1) for c, slot in keys]

    keys = list(slab_chunks)
    chunks = [slab_chunks[k] for k in keys]
    x = stack(chunks)
    x = across(x, 1)
    views = [block_view(c, block_rows) for c in chunks]
    cut = [i for i, k in enumerate(keys) if k[1] != here[-1]]
    rest = [i for i, k in enumerate(keys) if k[1] == here[-1]]
    restored = put_blocks(order, [views[i] for i in cut], [[keys[i]] for i in cut], owned, block_rows, slab_rows)
    views = [views[i] for i in rest] + [block_view(x, block_rows)]
    pieces = [[keys[i]] for i in rest] + [other(keys)]
    restored = put_blocks(order, views, pieces, owned, block_rows, slab_rows, [restored])

    keys = list(tied_chunks)
    early, late = [k for k in keys if k[1] != here[-1]], [k for k in keys if k[1] == here[-1]]
    chunks = [tied_chunks[k] for k in early]
    x = stack(chunks)
    x = across(x, 1)
    tied_full = put_groups([*chunks, x], [[k] for k in early] + [other(early)], group, tied_rows)
    chunks = [tied_chunks[k] for k in late]
    brought = []
    for (c, _), x in zip(late, chunks):
        brought.append(across(x, 1))
    pieces = [[k] for k in late] + [other([k]) for k in late]
    tied_full = put_groups([*chunks, *brought], pieces, group, tied_rows, [tied_full])

    return (*(x[None] for x in states[:3]), flat_view(restored)[None], *(x[None] for x in states[3:]), tied_full[None])


def solution(mesh):
    split = P("pipe", "dp", None)
    step = jax.shard_map(
        body,
        mesh=mesh,
        in_specs=(P("pipe", "dp", None, None), P("pipe", "dp", None, None), P("pipe", None), P("pipe")) + (split,) * 6,
        out_specs=(split, split, split, P("pipe", None, None), split, split, split, P("pipe", None, None)),
        check_vma=False,
    )
    if len(link_slots(mesh.shape["dp"])) != 4:
        return step
    return step
```
